32 devices in a mesh: win: 2 (over y), gz: 4 (over z), gy: 2 (over x), gx: 2 (over core).
Axes of the slice: x: 2, y: 2, z: 4, core: 2. Of those that a mesh axis runs over, the one named last changes fastest.
Arguments:
- noisy: float32 [32, 16, 256], P(('win', 'gz'), 'gy', 'gx'), parts along dimension 0, may hold values from -6 to 6
- first_weight: float32 [32, 1, 27], replicated, may hold values from -1.25 to 1.25
- first_bias: float32 [16], replicated, may hold values from -8 to -3
- second_weight: float32 [32, 16, 27], replicated, may hold values from -0.3125 to 0.3125
- second_bias: float32 [16], replicated, may hold values from -8 to -3
- head_weight: float32 [16], replicated, may hold values from -18 to 18
- seg_weight_in: float32 [16, 1, 27], replicated, may hold values from -1.25 to 1.25
- seg_bias_in: float32 [16], replicated, may hold values from -3 to 3
- seg_weight_out: float32 [16, 16, 27], replicated, may hold values from -0.3125 to 0.3125
- seg_bias_out: float32 [16], replicated, may hold values from -3 to 3
Outputs:
- denoised: float32 [32, 16, 256], P(('win', 'gz'), 'gy', 'gx'), parts along dimension 0
- segmented: float32 [16, 32, 16, 256], P(None, ('win', 'gz'), 'gy', 'gx'), parts along dimension 1
The draws below stay inside these ranges and needn't reach their ends.
There are 2 independent parts, one for each index of `win`. The reference program is written for one: setup_inputs(seed, part) draws one part's arguments, and reference() takes and returns one part's arrays. A program takes and returns all parts, laid end to end along the dimension named above; an argument that names none is the same for every part. Nothing has to cross between parts.
All inputs are finite; a program needn't handle non-finite values.
Results may differ from the reference program's by a relative error of at most 0.00029.
Values sent between devices are 32-bit elements; how exact they have to be, the bound alone decides.
A program may use at most 64 MiB of HBM per device.

```python
import jax
import jax.numpy as jnp
from jax import lax

C = 16
TAPS = 27
NZ = 16
NY = 16
NX = 256


def level_of(key, shape, pieces, low, high):
    level = 1.0
    for dim, shards_of in pieces:
        steps = jax.random.uniform(jax.random.fold_in(jax.random.fold_in(key, 6), dim), (shards_of,), jnp.float32, low / len(pieces), high / len(pieces))
        level = level * jnp.repeat(jnp.exp(steps), shape[dim] // shards_of).reshape((-1,) + (1,) * (len(shape) - 1 - dim))
    return level


def noise(stream_key, extent, width, limit, cuts=(), kind=jnp.bfloat16):
    drawn = jax.random.normal(stream_key, extent, jnp.float32) * width
    if len(cuts) > 0:
        drawn = level_of(stream_key, extent, cuts, -0.22, 0.18) * drawn
    return jnp.clip(drawn, min=-limit, max=limit).astype(kind)


def setup_inputs(seed: int = 0, part: int = 0) -> dict:
    key_of = jax.random.split(jax.random.key(seed), 11)
    part_splits = jax.random.split(jax.random.fold_in(key_of[10], part), 11)
    noisy = noise(part_splits[0], (NZ, NY, NX), 1.0, 6.0, ((0, 4), (1, 2), (2, 2)), jnp.float32)
    first_weight = noise(key_of[1], (2 * C, 1, TAPS), TAPS ** -0.5, 1.25, (), jnp.float32)
    first_bias = jnp.clip(jax.random.uniform(key_of[2], (C,), jnp.float32, -8.0, -3.0), -8.0, -3.0)
    second_weight = noise(key_of[3], (2 * C, C, TAPS), (C * TAPS) ** -0.5, 0.3125, (), jnp.float32)
    second_bias = jnp.clip(jax.random.uniform(key_of[4], (C,), jnp.float32, -8.0, -3.0), -8.0, -3.0)
    head_weight = noise(key_of[5], (C,), 3.0, 18.0, (), jnp.float32)
    seg_weight_in = noise(key_of[6], (C, 1, TAPS), TAPS ** -0.5, 1.25, (), jnp.float32)
    seg_bias_in = noise(key_of[7], (C,), 0.5, 3.0, (), jnp.float32)
    seg_weight_out = noise(key_of[8], (C, C, TAPS), (C * TAPS) ** -0.5, 0.3125, (), jnp.float32)
    seg_bias_out = noise(key_of[9], (C,), 0.5, 3.0, (), jnp.float32)
    return dict(noisy=noisy, first_weight=first_weight, first_bias=first_bias, second_weight=second_weight, second_bias=second_bias, head_weight=head_weight, seg_weight_in=seg_weight_in, seg_bias_in=seg_bias_in, seg_weight_out=seg_weight_out, seg_bias_out=seg_bias_out)


def convolve(field, weight):
    kernel = weight.reshape(weight.shape[0], weight.shape[1], 3, 3, 3)
    result = lax.conv_general_dilated(field[None], kernel, (1, 1, 1), ((1, 1), (1, 1), (1, 1)), dimension_numbers=("NCDHW", "OIDHW", "NCDHW"), precision=lax.Precision.HIGHEST)
    return result[0]


def recurrent(field, weight, bias, backward):
    channels = bias.shape[0]
    pre = convolve(field, weight)
    cand = jnp.tanh(pre[:channels])
    keep = jax.nn.sigmoid(-(pre[channels:] + bias[:, None, None, None]))
    inject = (1.0 - keep) * cand

    def advance(state, inputs):
        state = inputs[0] * state + inputs[1]
        return state, state

    start = jnp.zeros((channels, field.shape[2], field.shape[3]), jnp.float32)
    _, states = lax.scan(advance, start, (jnp.moveaxis(keep, 1, 0), jnp.moveaxis(inject, 1, 0)), reverse=backward)
    return jnp.moveaxis(states, 0, 1)


def reference(noisy, first_weight, first_bias, second_weight, second_bias, head_weight, seg_weight_in, seg_bias_in, seg_weight_out, seg_bias_out):
    first_hidden = recurrent(noisy[None], first_weight, first_bias, False)
    second_hidden = recurrent(first_hidden, second_weight, second_bias, True)
    denoised = noisy + jnp.einsum("c,czyx->zyx", head_weight, second_hidden, precision=lax.Precision.HIGHEST)
    features = jnp.maximum(convolve(denoised[None], seg_weight_in) + seg_bias_in[:, None, None, None], 0.0)
    segmented = convolve(features, seg_weight_out) + seg_bias_out[:, None, None, None]
    return denoised, segmented
```

```python
import functools

import jax
import jax.numpy as jnp
from jax import lax
from jax.experimental import pallas as pl
from jax.experimental.pallas import tpu as pltpu
from jax.sharding import PartitionSpec as P

LANES = 128
F32 = jnp.float32
BF16 = jnp.bfloat16
MESH = pl.DeviceIdType.MESH


def split(value):
    high = value.astype(BF16)
    return high, (value - high.astype(F32)).astype(BF16)


def left_rows(weight):
    high, low = split(weight)
    return jnp.concatenate([high, high, low], axis=1)


def right_rows(high, low):
    return jnp.concatenate([high, low, high], axis=0)


def mxu(left, right):
    return jnp.dot(left, right, preferred_element_type=F32)


def lane_of(shape):
    return lax.broadcasted_iota(jnp.int32, shape, len(shape) - 1)


def row_of(shape):
    return lax.broadcasted_iota(jnp.int32, shape, 0)


def times(count, step, carry, backward=False):
    if count <= 16:
        for i in range(count):
            carry = step(count - 1 - i if backward else i, carry)
        return carry
    return lax.fori_loop(0, count, lambda i, c: step(count - 1 - i if backward else i, c), carry)


def aligned(start, unit):
    return start if isinstance(start, int) else pl.multiple_of(start, unit)


def gather_kernel(sizes, noisy_ref, m1, x1, where_ref, m1_send, m1_recv, x1_send, x1_recv):
    gz, gy, gx = sizes
    me = lax.axis_index("gz")
    at_y = lax.axis_index("gy")
    at_x = lax.axis_index("gx")
    low_slab = me == 0
    high_slab = me == gz - 1

    def exists(dy, dx):
        ok = None
        for where, step, count in ((at_y, dy, gy), (at_x, dx, gx)):
            if step == 0:
                continue
            here = where > 0 if step < 0 else where < count - 1
            ok = here if ok is None else ok & here
        return ok

    def when(ok, action):
        if ok is None:
            action()
        else:
            pl.when(ok)(action)

    def device(z, dy, dx):
        return {
            "win": lax.axis_index("win"),
            "gz": z,
            "gy": lax.rem(at_y + dy + gy, gy),
            "gx": lax.rem(at_x + dx + gx, gx),
        }

    def block(z):
        return z

    def peer(k):
        return lax.rem(me + k, gz)

    steps_y = (0,) + ((-1, 1) if gy > 1 else ())
    steps_x = (0,) + ((-1, 1) if gx > 1 else ())

    barrier = pltpu.get_barrier_semaphore()
    for dy in steps_y:
        for dx in steps_x:
            for k in range(gz):
                if (dy, dx, k) != (0, 0, 0):
                    def greet(dy=dy, dx=dx, k=k):
                        pl.semaphore_signal(
                            barrier, inc=1, device_id=device(peer(k), dy, dx), device_id_type=MESH
                        )
                    when(exists(dy, dx), greet)
    span_y = 1 + (at_y > 0).astype(jnp.int32) + (at_y < gy - 1).astype(jnp.int32)
    span_x = 1 + (at_x > 0).astype(jnp.int32) + (at_x < gx - 1).astype(jnp.int32)
    pl.semaphore_wait(barrier, gz * span_y * span_x - 1)

    def noisy_middle(dy, k):
        target = peer(k)
        return pltpu.make_async_remote_copy(
            src_ref=noisy_ref,
            dst_ref=m1.at[1 - dy, block(me)],
            send_sem=m1_send.at[dy + 1, k],
            recv_sem=m1_recv.at[1 - dy, me],
            device_id=device(target, dy, 0),
            device_id_type=MESH,
        )

    def noisy_edge(dy, dx):
        target = 0 if dx > 0 else gz - 1
        side = (dx + 1) // 2
        return pltpu.make_async_remote_copy(
            src_ref=noisy_ref,
            dst_ref=x1.at[1 - dy, block(me)],
            send_sem=x1_send.at[dy + 1, side],
            recv_sem=x1_recv.at[1 - dy, me],
            device_id=device(target, dy, dx),
            device_id_type=MESH,
        )

    sends = []
    for dy in steps_y:
        for k in range(gz - 1, -1, -1):
            if (dy, k) != (0, 0):
                sends.append((exists(dy, 0), functools.partial(noisy_middle, dy, k)))
    for dy in steps_y:
        for dx in steps_x:
            if dx != 0:
                sends.append((exists(dy, dx), functools.partial(noisy_edge, dy, dx)))
    for ok, make in sends:
        when(ok, lambda make=make: make().start())

    for i, value in enumerate((me, at_y, at_x)):
        where_ref[i] = value
    m1[1, block(me)] = noisy_ref[...]
    for index, ok in ((0, at_y == 0), (2, at_y == gy - 1)):
        def no_row(index=index):
            for z in range(gz):
                m1[index, z] = jnp.zeros(m1.shape[2:], F32)
                x1[index, z] = jnp.zeros(x1.shape[2:], F32)
        pl.when(ok)(no_row)
    no_edge = jnp.logical_not((low_slab & (at_x > 0)) | (high_slab & (at_x < gx - 1)))

    def no_neighbour():
        x1[...] = jnp.zeros(x1.shape, F32)

    pl.when(no_edge)(no_neighbour)
    for dy in steps_y:
        for k in range(gz):
            if (dy, k) != (0, 0):
                source = peer(k)
                def await_middle(dy=dy, source=source):
                    pltpu.make_async_remote_copy(
                        src_ref=noisy_ref,
                        dst_ref=m1.at[1 + dy, block(source)],
                        send_sem=m1_send.at[1 + dy, 0],
                        recv_sem=m1_recv.at[1 + dy, source],
                        device_id=device(source, dy, 0),
                        device_id_type=MESH,
                    ).wait_recv()
                when(exists(dy, 0), await_middle)
    for dy in steps_y:
        for dx in steps_x:
            if dx != 0:
                ok = exists(dy, dx) & (low_slab if dx < 0 else high_slab)
                for source in range(gz):
                    def await_edge(dy=dy, dx=dx, source=source):
                        pltpu.make_async_remote_copy(
                            src_ref=noisy_ref,
                            dst_ref=x1.at[1 + dy, block(source)],
                            send_sem=x1_send.at[1 + dy, 0],
                            recv_sem=x1_recv.at[1 + dy, source],
                            device_id=device(source, dy, dx),
                            device_id_type=MESH,
                        ).wait_recv()
                    pl.when(ok)(await_edge)

    for ok, make in sends:
        when(ok, lambda make=make: make().wait_send())


def layers_kernel(
    sizes, shape, where_ref, m1, x1, narrow_ref, wide_ref, bias_ref, packed, taps, taps_high, taps_low, product, fix
):
    gz, gy, gx = sizes
    bz, by, bx = shape
    depth = gz * bz
    slab = bx // gz
    out_lanes = by * slab
    tiles = taps.shape[0]
    me, at_y, at_x = where_ref[0], where_ref[1], where_ref[2]
    low_slab = me == 0
    high_slab = me == gz - 1
    taps[...] = jnp.zeros(taps.shape, F32)
    for plane in (0, depth + 1):
        product[plane] = jnp.zeros(product.shape[1:], F32)
    fix[...] = jnp.zeros(fix.shape, F32)
    first_left = left_rows(narrow_ref[0:96, :])
    second_left = left_rows(
        jnp.concatenate([wide_ref[48 * a : 48 * a + 32, :] for a in range(3)], axis=0)
    )
    first_bias = bias_ref[:, 0:1]
    second_bias = bias_ref[0:16, 1:2]
    head = bias_ref[0:16, 2:3]
    shape = (48, tiles * LANES)
    lane, row = lane_of(shape), row_of(shape)
    place_y = at_y * by + lane // slab - 1
    place_x = at_x * bx + me * slab + lane % slab + row // 16 - 1
    inside = (place_y >= 0) & (place_y < gy * by) & (place_x >= 0) & (place_x < gx * bx)
    mask = jnp.where(inside, 1.0, 0.0).astype(F32)

    lane = lane_of((depth, LANES))
    take_edge = (low_slab & (lane >= bx - 2)) | (high_slab & (lane < 2))
    windows = []
    turn = lax.rem(2 - me * slab + bx, bx)
    for line in range(by + 4):
        index, y = (0, by - 2 + line) if line < 2 else (1, line - 2) if line < by + 2 else (2, line - by - 2)
        rows = []
        for source in (m1, x1):
            rows.append(source[index, pl.ds(y, depth, stride=by), :])
        windows.append(pltpu.roll(jnp.where(take_edge, rows[1], rows[0]), turn, 1))
    wide_tiles = -(-(by + 4) * slab // LANES)
    for s in range(5):
        strips = []
        for tile in range(wide_tiles):
            strip = jnp.zeros((depth, LANES), F32)
            for line in range(by + 4):
                if line * slab // LANES == tile:
                    begin = line * slab % LANES
                    piece = pltpu.roll(windows[line], (begin - s) % LANES, 1)
                    strip = jnp.where((lane >= begin) & (lane < begin + slab), piece, strip)
            strips.append(strip)
        strips.append(jnp.zeros((depth, LANES), F32))
        for b in range(3):
            for tile in range(tiles):
                jump, off = divmod(b * slab, LANES)
                value = strips[min(tile + jump, wide_tiles)]
                if off:
                    after = strips[min(tile + jump + 1, wide_tiles)]
                    value = jnp.where(
                        lane < LANES - off,
                        pltpu.roll(value, LANES - off, 1),
                        pltpu.roll(after, LANES - off, 1),
                    )
                taps[tile, pl.ds(16 + b * 5 + s, depth, stride=16), :] = value
    high, low = split(taps[...])
    taps_high[...] = high
    taps_low[...] = low

    def forward(z, hidden):
        rows = pl.ds(aligned(z * 16, 16), 48)
        high = jnp.concatenate([taps_high[t, rows, :] for t in range(tiles)], axis=1)
        low = jnp.concatenate([taps_low[t, rows, :] for t in range(tiles)], axis=1)
        pre = mxu(first_left, right_rows(high, low))
        cand = jnp.tanh(pre[0:48])
        change = jax.nn.sigmoid(pre[48:96] + first_bias)
        hidden = hidden + change * (mask * cand - hidden)
        field = jnp.concatenate(
            [hidden[:, b * slab : b * slab + out_lanes] for b in range(3)], axis=0
        )
        high, low = split(field)
        product[z + 1] = mxu(second_left, right_rows(high, low))
        return hidden

    times(depth, forward, jnp.zeros((48, tiles * LANES), F32))

    def back(z, hidden):
        pre = product[z, 0:32] + product[z + 1, 32:64] + product[z + 2, 64:96]
        cand = jnp.tanh(pre[0:16])
        change = jax.nn.sigmoid(pre[16:32] + second_bias)
        hidden = hidden + change * (cand - hidden)
        fix[pl.ds(z + 2, 1), 0:out_lanes] = jnp.sum(head * hidden, axis=0, keepdims=True)
        return hidden

    times(depth, back, jnp.zeros((16, out_lanes), F32), True)
    for tile in range(-(-out_lanes // LANES)):
        lanes = slice(tile * LANES, (tile + 1) * LANES)
        centre = taps[tile, pl.ds(16 + 12, depth, stride=16), :]
        fix[2 : 2 + depth, lanes] = fix[2 : 2 + depth, lanes] + centre
    for target in range(gz):
        packed[target] = fix[bz * target : bz * target + bz + 4, :]


def scatter_kernel(sizes, packed, m3, x3, m3_send, m3_recv, x3_send, x3_recv):
    gz, gy, gx = sizes
    me = lax.axis_index("gz")
    at_y = lax.axis_index("gy")
    at_x = lax.axis_index("gx")
    low_slab = me == 0
    high_slab = me == gz - 1

    def exists(dy, dx):
        ok = None
        for where, step, count in ((at_y, dy, gy), (at_x, dx, gx)):
            if step == 0:
                continue
            here = where > 0 if step < 0 else where < count - 1
            ok = here if ok is None else ok & here
        return ok

    def when(ok, action):
        if ok is None:
            action()
        else:
            pl.when(ok)(action)

    def device(z, dy, dx):
        return {
            "win": lax.axis_index("win"),
            "gz": z,
            "gy": lax.rem(at_y + dy + gy, gy),
            "gx": lax.rem(at_x + dx + gx, gx),
        }

    def peer(k):
        return lax.rem(me + k, gz)

    steps_y = (0,) + ((-1, 1) if gy > 1 else ())
    steps_x = (0,) + ((-1, 1) if gx > 1 else ())

    barrier = pltpu.get_barrier_semaphore()
    for dy in steps_y:
        for dx in steps_x:
            for k in range(gz):
                if (dy, dx, k) != (0, 0, 0):
                    def greet(dy=dy, dx=dx, k=k):
                        pl.semaphore_signal(
                            barrier, inc=1, device_id=device(peer(k), dy, dx), device_id_type=MESH
                        )
                    when(exists(dy, dx), greet)
    span_y = 1 + (at_y > 0).astype(jnp.int32) + (at_y < gy - 1).astype(jnp.int32)
    span_x = 1 + (at_x > 0).astype(jnp.int32) + (at_x < gx - 1).astype(jnp.int32)
    pl.semaphore_wait(barrier, gz * span_y * span_x - 1)

    def clean_middle(dy, k):
        target = peer(k)
        return pltpu.make_async_remote_copy(
            src_ref=packed.at[target],
            dst_ref=m3.at[1 - dy, me],
            send_sem=m3_send.at[dy + 1, k],
            recv_sem=m3_recv.at[1 - dy, me],
            device_id=device(target, dy, 0),
            device_id_type=MESH,
        )

    def clean_edge(dy, dx, k):
        target = peer(k)
        side = (dx + 1) // 2
        return pltpu.make_async_remote_copy(
            src_ref=packed.at[target],
            dst_ref=x3.at[1 - dy, 1 - side],
            send_sem=x3_send.at[dy + 1, side, k],
            recv_sem=x3_recv.at[1 - dy, 1 - side],
            device_id=device(target, dy, dx),
            device_id_type=MESH,
        )

    late = []
    for dy in steps_y:
        for k in range(gz - 1, -1, -1):
            if (dy, k) != (0, 0):
                late.append((exists(dy, 0), functools.partial(clean_middle, dy, k)))
    for dy in steps_y:
        for dx in steps_x:
            if dx != 0:
                ok = exists(dy, dx) & (high_slab if dx > 0 else low_slab)
                for k in range(gz):
                    late.append((ok, functools.partial(clean_edge, dy, dx, k)))
    for ok, make in late:
        when(ok, lambda make=make: make().start())
    m3[1, me] = packed[me]
    for index, ok in ((0, at_y == 0), (2, at_y == gy - 1)):
        def no_row_again(index=index):
            m3[index] = jnp.zeros(m3.shape[1:], F32)
            x3[index] = jnp.zeros(x3.shape[1:], F32)
        pl.when(ok)(no_row_again)
    for side, ok in ((0, at_x == 0), (1, at_x == gx - 1)):
        def no_side(side=side):
            for index in range(3):
                x3[index, side] = jnp.zeros(x3.shape[2:], F32)
        pl.when(ok)(no_side)
    for dy in steps_y:
        for k in range(gz):
            if (dy, k) != (0, 0):
                source = peer(k)
                def await_clean(dy=dy, source=source):
                    pltpu.make_async_remote_copy(
                        src_ref=packed.at[0],
                        dst_ref=m3.at[1 + dy, source],
                        send_sem=m3_send.at[1 + dy, 0],
                        recv_sem=m3_recv.at[1 + dy, source],
                        device_id=device(source, dy, 0),
                        device_id_type=MESH,
                    ).wait_recv()
                when(exists(dy, 0), await_clean)
    for dy in steps_y:
        for dx in steps_x:
            if dx != 0:
                side = (dx + 1) // 2
                source = gz - 1 if dx < 0 else 0
                def await_side(dy=dy, dx=dx, side=side, source=source):
                    pltpu.make_async_remote_copy(
                        src_ref=packed.at[0],
                        dst_ref=x3.at[1 + dy, side],
                        send_sem=x3_send.at[1 + dy, side, 0],
                        recv_sem=x3_recv.at[1 + dy, side],
                        device_id=device(source, dy, dx),
                        device_id_type=MESH,
                    ).wait_recv()
                when(exists(dy, dx), await_side)

    for ok, make in late:
        when(ok, lambda make=make: make().wait_send())


def segment_kernel(
    sizes,
    where_ref,
    m3,
    x3,
    narrow_ref,
    wide_ref,
    bias_ref,
    clean_ref,
    out_ref,
    middle_ref,
    edge_ref,
    taps,
    result,
):
    gz, gy, gx = sizes
    lines, planes, bx = middle_ref.shape
    by, bz = lines - 4, planes - 4
    me, at_y, at_x = where_ref[0], where_ref[1], where_ref[2]
    slab = bx // gz
    lane = lane_of((bz + 4, LANES))
    for line in range(by + 4):
        index, y = (0, by - 2 + line) if line < 2 else (1, line - 2) if line < by + 2 else (2, line - by - 2)
        tile, off = divmod(y * slab, LANES)
        lanes = slice(tile * LANES, (tile + 1) * LANES)
        whole = jnp.zeros((bz + 4, LANES), F32)
        for source in range(gz):
            begin = source * slab
            piece = pltpu.roll(m3[index, source, :, lanes], (begin - off) % LANES, 1)
            whole = jnp.where((lane >= begin) & (lane < begin + slab), piece, whole)
        middle_ref[line] = whole
        before = pltpu.roll(x3[index, 0, :, lanes], (bx - off - slab) % LANES, 1)
        after = pltpu.roll(x3[index, 1, :, lanes], (-off) % LANES, 1)
        edge_ref[line] = jnp.where(lane < LANES // 2, after, before)

    in_left = left_rows(narrow_ref[96:144, :])
    out_left = left_rows(
        jnp.concatenate([wide_ref[48 * a + 32 : 48 * a + 48, :] for a in range(3)], axis=0)
    )
    in_bias = bias_ref[:, 3:4]
    out_bias = bias_ref[0:16, 4:5]
    for y in range(by + 2):
        taps[y, pl.ds(15, planes, stride=16), :] = jnp.zeros((planes, bx), F32)
    lane = lane_of((planes, bx))
    for line in range(lines):
        middle, edge = middle_ref[line], edge_ref[line]
        for s in range(5):
            value = middle
            if s < 2:
                value = pltpu.roll(jnp.where(lane >= bx - (2 - s), edge, middle), 2 - s, 1)
            if s > 2:
                value = pltpu.roll(jnp.where(lane < s - 2, edge, middle), bx - (s - 2), 1)
            for b in range(3):
                if 0 <= line - b < by + 2:
                    taps[line - b, pl.ds(b * 5 + s, planes, stride=16), :] = value

    for z in range(bz):
        clean_ref[z] = middle_ref[2 : 2 + by, 2 + z, :]
    shape = (48, (by + 2) * bx)
    lane, row = lane_of(shape), row_of(shape)
    place_y = at_y * by + lane // bx - 1
    place_x = at_x * bx + lane % bx + row // 16 - 1
    inside = (place_y >= 0) & (place_y < gy * by) & (place_x >= 0) & (place_x < gx * bx)
    mask = jnp.where(inside, 1.0, 0.0).astype(F32)
    partial = []
    for z in range(bz + 2):
        rows = jnp.concatenate([taps[y, z * 16 : z * 16 + 48, :] for y in range(by + 2)], axis=1)
        high, low = split(rows)
        grown = jnp.maximum(mxu(in_left, right_rows(high, low)) + in_bias, 0.0) * mask
        if z == 0:
            grown = grown * jnp.where(me > 0, 1.0, 0.0).astype(F32)
        if z == bz + 1:
            grown = grown * jnp.where(me < gz - 1, 1.0, 0.0).astype(F32)
        high, low = split(grown)
        field_high = jnp.concatenate([high[:, b * bx : (b + by) * bx] for b in range(3)], axis=0)
        field_low = jnp.concatenate([low[:, b * bx : (b + by) * bx] for b in range(3)], axis=0)
        partial.append(mxu(out_left, right_rows(field_high, field_low)))
        if z >= 2:
            total = partial[z - 2][0:16] + partial[z - 1][16:32] + partial[z][32:48] + out_bias
            for y in range(by):
                result[pl.ds((z - 2) * by + y, 16, stride=bz * by), :] = total[:, y * bx : (y + 1) * bx]
    out_ref[...] = result[0 : 16 * bz * by, :]


def narrow_rows(weight):
    parts = weight.shape[0] // 16
    kernel = weight.reshape(parts, 16, 3, 3, 3)
    moved = jnp.stack(
        [jnp.pad(kernel, ((0, 0),) * 4 + ((c, 2 - c),)) for c in range(3)], axis=1
    ).reshape(parts * 48, 3, 15)
    return jnp.pad(moved, ((0, 0), (0, 0), (0, 1))).reshape(parts * 48, 48)


def wide_rows(weight):
    outs, ins = weight.shape[0], weight.shape[1]
    return weight.reshape(outs, ins, 3, 9).transpose(2, 0, 3, 1).reshape(3 * outs, 9 * ins)


def body(sizes, noisy, first_weight, first_bias, second_weight, second_bias, head_weight,
         seg_weight_in, seg_bias_in, seg_weight_out, seg_bias_out):
    gz, gy, gx = sizes
    bz, by, bx = noisy.shape
    depth = gz * bz
    slab = bx // gz
    tiles = -(-(by + 2) * slab // LANES)
    out_lanes = by * slab
    out_tiles = -(-out_lanes // LANES)
    narrow = narrow_rows(jnp.concatenate([first_weight, seg_weight_in], axis=0))
    wide = wide_rows(jnp.concatenate([second_weight, seg_weight_out], axis=0))
    biases = jnp.stack([first_bias, second_bias, head_weight, seg_bias_in, seg_bias_out], axis=1)
    biases = jnp.tile(biases, (3, 1))
    vmem = pl.BlockSpec(memory_space=pltpu.VMEM)
    dma = pltpu.SemaphoreType.DMA
    smem = pl.BlockSpec(memory_space=pltpu.SMEM)
    blocks = jax.ShapeDtypeStruct((3, gz, bz * by, bx), F32)
    m1, x1, where = pl.pallas_call(
        functools.partial(gather_kernel, sizes),
        out_shape=[blocks, blocks, jax.ShapeDtypeStruct((3,), jnp.int32)],
        in_specs=[vmem],
        out_specs=[vmem, vmem, smem],
        scratch_shapes=[dma((3, gz)), dma((3, gz)), dma((3, 2)), dma((3, gz))],
        compiler_params=pltpu.CompilerParams(collective_id=0, has_side_effects=True),
        name="gather",
    )(noisy.reshape(bz * by, bx))
    packed = pl.pallas_call(
        functools.partial(layers_kernel, sizes, (bz, by, bx)),
        out_shape=jax.ShapeDtypeStruct((gz, bz + 4, out_tiles * LANES), F32),
        in_specs=[smem] + [vmem] * 5,
        out_specs=vmem,
        scratch_shapes=[
            pltpu.VMEM((tiles, (depth + 2) * 16, LANES), F32),
            pltpu.VMEM((tiles, (depth + 2) * 16, LANES), BF16),
            pltpu.VMEM((tiles, (depth + 2) * 16, LANES), BF16),
            pltpu.VMEM((depth + 2, 96, out_lanes), F32),
            pltpu.VMEM((depth + 16, out_tiles * LANES), F32),
        ],
        name="layers",
    )(where, m1.reshape(3, depth * by, bx), x1.reshape(3, depth * by, bx), narrow, wide, biases)
    m3, x3 = pl.pallas_call(
        functools.partial(scatter_kernel, sizes),
        out_shape=[
            jax.ShapeDtypeStruct((3, gz, bz + 4, out_tiles * LANES), F32),
            jax.ShapeDtypeStruct((3, 2, bz + 4, out_tiles * LANES), F32),
        ],
        in_specs=[vmem],
        out_specs=[vmem] * 2,
        scratch_shapes=[dma((3, gz)), dma((3, gz)), dma((3, 2, gz)), dma((3, 2))],
        compiler_params=pltpu.CompilerParams(collective_id=1, has_side_effects=True),
        name="scatter",
    )(packed)
    clean, features = pl.pallas_call(
        functools.partial(segment_kernel, sizes),
        out_shape=[
            jax.ShapeDtypeStruct((bz, by, bx), F32),
            jax.ShapeDtypeStruct((16 * bz * by, bx), F32),
        ],
        in_specs=[smem] + [vmem] * 5,
        out_specs=[vmem] * 2,
        scratch_shapes=[
            pltpu.VMEM((by + 4, bz + 4, bx), F32),
            pltpu.VMEM((by + 4, bz + 4, bx), F32),
            pltpu.VMEM((by + 2, (bz + 5) * 16, bx), F32),
            pltpu.VMEM((17 * bz * by, bx), F32),
        ],
        name="segment",
    )(where, m3, x3, narrow, wide, biases)
    return clean, features.reshape(16, bz, by, bx)


def solution(mesh):
    sizes = (mesh.shape["gz"], mesh.shape["gy"], mesh.shape["gx"])
    in_specs = (P(("win", "gz"), "gy", "gx"), P(), P(), P(), P(), P(), P(), P(), P(), P())
    out_specs = (P(("win", "gz"), "gy", "gx"), P(None, ("win", "gz"), "gy", "gx"))
    return jax.shard_map(
        functools.partial(body, sizes), mesh=mesh, in_specs=in_specs, out_specs=out_specs, check_vma=False
    )
```

```python
import functools

import jax
import jax.numpy as jnp
from jax import lax
from jax.experimental import pallas as pl
from jax.experimental.pallas import tpu as pltpu
from jax.sharding import PartitionSpec as P

LANES = 128
F32 = jnp.float32
BF16 = jnp.bfloat16
MESH = pl.DeviceIdType.MESH


def split(value):
    high = value.astype(BF16)
    return high, (value - high.astype(F32)).astype(BF16)


def left_rows(weight):
    high, low = split(weight)
    return jnp.concatenate([high, high, low], axis=1)


def right_rows(high, low):
    return jnp.concatenate([high, low, high], axis=0)


def mxu(left, right):
    return jnp.dot(left, right, preferred_element_type=F32)


def lane_of(shape):
    return lax.broadcasted_iota(jnp.int32, shape, len(shape) - 1)


def row_of(shape):
    return lax.broadcasted_iota(jnp.int32, shape, 0)


def column(row_ref):
    count = row_ref.shape[1]
    shape = (count, count)
    spread = jnp.broadcast_to(row_ref[...], shape)
    return jnp.sum(jnp.where(row_of(shape) == lane_of(shape), spread, 0.0), axis=1, keepdims=True)


def times(count, step, carry, backward=False):
    if count <= 16:
        for i in range(count):
            carry = step(count - 1 - i if backward else i, carry)
        return carry
    return lax.fori_loop(0, count, lambda i, c: step(count - 1 - i if backward else i, c), carry)


def aligned(start, unit):
    return start if isinstance(start, int) else pl.multiple_of(start, unit)


def gather_kernel(sizes, by, noisy_ref, m1, x1, my, xy, where_ref, halo, m1_send, m1_recv, x1_send, x1_recv):
    gz, gy, gx = sizes
    me = lax.axis_index("gz")
    at_y = lax.axis_index("gy")
    at_x = lax.axis_index("gx")
    low_slab = me == 0
    high_slab = me == gz - 1

    def exists(dy, dx):
        ok = None
        for where, step, count in ((at_y, dy, gy), (at_x, dx, gx)):
            if step == 0:
                continue
            here = where > 0 if step < 0 else where < count - 1
            ok = here if ok is None else ok & here
        return ok

    def when(ok, action):
        if ok is None:
            action()
        else:
            pl.when(ok)(action)

    def device(z, dy, dx):
        return {
            "win": lax.axis_index("win"),
            "gz": z,
            "gy": lax.rem(at_y + dy + gy, gy),
            "gx": lax.rem(at_x + dx + gx, gx),
        }

    def peer(k):
        return lax.rem(me + k, gz)

    steps_y = (0,) + ((-1, 1) if gy > 1 else ())
    steps_x = (0,) + ((-1, 1) if gx > 1 else ())

    for side, first in ((0, 0), (1, by - 2)):
        for z in range(noisy_ref.shape[0] // by):
            halo[side, 2 * z : 2 * z + 2, :] = noisy_ref[z * by + first : z * by + first + 2, :]

    def payload(dy):
        return noisy_ref if dy == 0 else halo.at[(dy + 1) // 2]

    def slot(edge, dy, z):
        if dy == 0:
            return (x1 if edge else m1).at[z]
        return (xy if edge else my).at[(dy + 1) // 2, z]

    barrier = pltpu.get_barrier_semaphore()
    for dy in steps_y:
        for dx in steps_x:
            for k in range(gz):
                if (dy, dx, k) != (0, 0, 0):
                    def greet(dy=dy, dx=dx, k=k):
                        pl.semaphore_signal(
                            barrier, inc=1, device_id=device(peer(k), dy, dx), device_id_type=MESH
                        )
                    when(exists(dy, dx), greet)
    span_y = 1 + (at_y > 0).astype(jnp.int32) + (at_y < gy - 1).astype(jnp.int32)
    span_x = 1 + (at_x > 0).astype(jnp.int32) + (at_x < gx - 1).astype(jnp.int32)
    pl.semaphore_wait(barrier, gz * span_y * span_x - 1)

    def noisy_middle(dy, k):
        target = peer(k)
        return pltpu.make_async_remote_copy(
            src_ref=payload(dy),
            dst_ref=slot(False, -dy, me),
            send_sem=m1_send.at[dy + 1, k],
            recv_sem=m1_recv.at[1 - dy, me],
            device_id=device(target, dy, 0),
            device_id_type=MESH,
        )

    def noisy_edge(dy, dx):
        target = 0 if dx > 0 else gz - 1
        side = (dx + 1) // 2
        return pltpu.make_async_remote_copy(
            src_ref=payload(dy),
            dst_ref=slot(True, -dy, me),
            send_sem=x1_send.at[dy + 1, side],
            recv_sem=x1_recv.at[1 - dy, me],
            device_id=device(target, dy, dx),
            device_id_type=MESH,
        )

    sends = []
    for dy in steps_y:
        for k in range(gz - 1, -1, -1):
            if (dy, k) != (0, 0):
                sends.append((exists(dy, 0), functools.partial(noisy_middle, dy, k)))
    for dy in steps_y:
        for dx in steps_x:
            if dx != 0:
                sends.append((exists(dy, dx), functools.partial(noisy_edge, dy, dx)))
    for ok, make in sends:
        when(ok, lambda make=make: make().start())

    for i, value in enumerate((me, at_y, at_x)):
        where_ref[i] = value
    m1[me] = noisy_ref[...]
    for index, ok in ((0, at_y == 0), (1, at_y == gy - 1)):
        def no_row(index=index):
            for z in range(gz):
                my[index, z] = jnp.zeros(my.shape[2:], F32)
                xy[index, z] = jnp.zeros(xy.shape[2:], F32)
        pl.when(ok)(no_row)
    no_edge = jnp.logical_not((low_slab & (at_x > 0)) | (high_slab & (at_x < gx - 1)))

    def no_neighbour():
        x1[...] = jnp.zeros(x1.shape, F32)
        xy[...] = jnp.zeros(xy.shape, F32)

    pl.when(no_edge)(no_neighbour)
    for dy in steps_y:
        for k in range(gz):
            if (dy, k) != (0, 0):
                source = peer(k)
                def await_middle(dy=dy, source=source):
                    pltpu.make_async_remote_copy(
                        src_ref=payload(dy),
                        dst_ref=slot(False, dy, source),
                        send_sem=m1_send.at[1 + dy, 0],
                        recv_sem=m1_recv.at[1 + dy, source],
                        device_id=device(source, dy, 0),
                        device_id_type=MESH,
                    ).wait_recv()
                when(exists(dy, 0), await_middle)
    for dy in steps_y:
        for dx in steps_x:
            if dx != 0:
                ok = exists(dy, dx) & (low_slab if dx < 0 else high_slab)
                for source in range(gz):
                    def await_edge(dy=dy, dx=dx, source=source):
                        pltpu.make_async_remote_copy(
                            src_ref=payload(dy),
                            dst_ref=slot(True, dy, source),
                            send_sem=x1_send.at[1 + dy, 0],
                            recv_sem=x1_recv.at[1 + dy, source],
                            device_id=device(source, dy, dx),
                            device_id_type=MESH,
                        ).wait_recv()
                    pl.when(ok)(await_edge)

    for ok, make in sends:
        when(ok, lambda make=make: make().wait_send())


def layers_kernel(
    sizes, shape, where_ref, m1, x1, my, xy, narrow_ref, wide_ref, first_ref, second_ref, head_ref, packed, taps, taps_high, taps_low, product, fix
):
    gz, gy, gx = sizes
    bz, by, bx = shape
    depth = gz * bz
    slab = bx // gz
    out_lanes = by * slab
    tiles = taps.shape[0]
    me, at_y, at_x = where_ref[0], where_ref[1], where_ref[2]
    low_slab = me == 0
    high_slab = me == gz - 1
    taps[...] = jnp.zeros(taps.shape, F32)
    for plane in (0, depth + 1):
        product[plane] = jnp.zeros(product.shape[1:], F32)
    fix[...] = jnp.zeros(fix.shape, F32)
    first_left = left_rows(narrow_ref[0:96, :])
    second_left = left_rows(
        jnp.concatenate([wide_ref[48 * a : 48 * a + 32, :] for a in range(3)], axis=0)
    )
    first_bias = jnp.concatenate([column(first_ref)] * 3, axis=0)
    second_bias = column(second_ref)
    head = column(head_ref)
    shape = (48, tiles * LANES)
    lane, row = lane_of(shape), row_of(shape)
    place_y = at_y * by + lane // slab - 1
    place_x = at_x * bx + me * slab + lane % slab + row // 16 - 1
    inside = (place_y >= 0) & (place_y < gy * by) & (place_x >= 0) & (place_x < gx * bx)
    mask = jnp.where(inside, 1.0, 0.0).astype(F32)

    lane = lane_of((depth, LANES))
    take_edge = (low_slab & (lane >= bx - 2)) | (high_slab & (lane < 2))
    windows = []
    turn = lax.rem(2 - me * slab + bx, bx)
    for line in range(by + 4):
        rows = []
        for source, beside in ((m1, my), (x1, xy)):
            if 2 <= line < by + 2:
                rows.append(source[pl.ds(line - 2, depth, stride=by), :])
            else:
                side, place = (0, line) if line < 2 else (1, line - by - 2)
                rows.append(beside[side, pl.ds(place, depth, stride=2), :])
        windows.append(pltpu.roll(jnp.where(take_edge, rows[1], rows[0]), turn, 1))
    wide_tiles = -(-(by + 4) * slab // LANES)
    for s in range(5):
        strips = []
        for tile in range(wide_tiles):
            strip = jnp.zeros((depth, LANES), F32)
            for line in range(by + 4):
                if line * slab // LANES == tile:
                    begin = line * slab % LANES
                    piece = pltpu.roll(windows[line], (begin - s) % LANES, 1)
                    strip = jnp.where((lane >= begin) & (lane < begin + slab), piece, strip)
            strips.append(strip)
        strips.append(jnp.zeros((depth, LANES), F32))
        for b in range(3):
            for tile in range(tiles):
                jump, off = divmod(b * slab, LANES)
                value = strips[min(tile + jump, wide_tiles)]
                if off:
                    after = strips[min(tile + jump + 1, wide_tiles)]
                    value = jnp.where(
                        lane < LANES - off,
                        pltpu.roll(value, LANES - off, 1),
                        pltpu.roll(after, LANES - off, 1),
                    )
                taps[tile, pl.ds(16 + b * 5 + s, depth, stride=16), :] = value
    high, low = split(taps[...])
    taps_high[...] = high
    taps_low[...] = low

    def forward(z, hidden):
        rows = pl.ds(aligned(z * 16, 16), 48)
        high = jnp.concatenate([taps_high[t, rows, :] for t in range(tiles)], axis=1)
        low = jnp.concatenate([taps_low[t, rows, :] for t in range(tiles)], axis=1)
        pre = mxu(first_left, right_rows(high, low))
        cand = jnp.tanh(pre[0:48])
        change = jax.nn.sigmoid(pre[48:96] + first_bias)
        hidden = hidden + change * (mask * cand - hidden)
        field = jnp.concatenate(
            [hidden[:, b * slab : b * slab + out_lanes] for b in range(3)], axis=0
        )
        high, low = split(field)
        product[z + 1] = mxu(second_left, right_rows(high, low))
        return hidden

    times(depth, forward, jnp.zeros((48, tiles * LANES), F32))

    def back(z, hidden):
        pre = product[z, 0:32] + product[z + 1, 32:64] + product[z + 2, 64:96]
        cand = jnp.tanh(pre[0:16])
        change = jax.nn.sigmoid(pre[16:32] + second_bias)
        hidden = hidden + change * (cand - hidden)
        fix[pl.ds(z + 2, 1), 0:out_lanes] = jnp.sum(head * hidden, axis=0, keepdims=True)
        return hidden

    times(depth, back, jnp.zeros((16, out_lanes), F32), True)
    for tile in range(-(-out_lanes // LANES)):
        lanes = slice(tile * LANES, (tile + 1) * LANES)
        centre = taps[tile, pl.ds(16 + 12, depth, stride=16), :]
        fix[2 : 2 + depth, lanes] = fix[2 : 2 + depth, lanes] + centre
    for target in range(gz):
        packed[target] = fix[bz * target : bz * target + bz + 4, :]


def scatter_kernel(sizes, by, slab, packed, m3, x3, m3_send, m3_recv, x3_send, x3_recv):
    gz, gy, gx = sizes
    me = lax.axis_index("gz")
    at_y = lax.axis_index("gy")
    at_x = lax.axis_index("gx")
    low_slab = me == 0
    high_slab = me == gz - 1

    def exists(dy, dx):
        ok = None
        for where, step, count in ((at_y, dy, gy), (at_x, dx, gx)):
            if step == 0:
                continue
            here = where > 0 if step < 0 else where < count - 1
            ok = here if ok is None else ok & here
        return ok

    def when(ok, action):
        if ok is None:
            action()
        else:
            pl.when(ok)(action)

    def device(z, dy, dx):
        return {
            "win": lax.axis_index("win"),
            "gz": z,
            "gy": lax.rem(at_y + dy + gy, gy),
            "gx": lax.rem(at_x + dx + gx, gx),
        }

    def peer(k):
        return lax.rem(me + k, gz)

    steps_y = (0,) + ((-1, 1) if gy > 1 else ())
    steps_x = (0,) + ((-1, 1) if gx > 1 else ())

    barrier = pltpu.get_barrier_semaphore()
    for dy in steps_y:
        for dx in steps_x:
            for k in range(gz):
                if (dy, dx, k) != (0, 0, 0):
                    def greet(dy=dy, dx=dx, k=k):
                        pl.semaphore_signal(
                            barrier, inc=1, device_id=device(peer(k), dy, dx), device_id_type=MESH
                        )
                    when(exists(dy, dx), greet)
    span_y = 1 + (at_y > 0).astype(jnp.int32) + (at_y < gy - 1).astype(jnp.int32)
    span_x = 1 + (at_x > 0).astype(jnp.int32) + (at_x < gx - 1).astype(jnp.int32)
    pl.semaphore_wait(barrier, gz * span_y * span_x - 1)

    lanes = packed.shape[2]
    last = (by - 2) * slab // LANES * LANES

    def part(dy):
        return {0: slice(0, lanes), 1: slice(last, last + LANES), -1: slice(0, LANES)}[dy]

    def clean_middle(dy, k):
        target = peer(k)
        return pltpu.make_async_remote_copy(
            src_ref=packed.at[target, :, part(dy)],
            dst_ref=m3.at[1 - dy, me, :, part(dy)],
            send_sem=m3_send.at[dy + 1, k],
            recv_sem=m3_recv.at[1 - dy, me],
            device_id=device(target, dy, 0),
            device_id_type=MESH,
        )

    def clean_edge(dy, dx, k):
        target = peer(k)
        side = (dx + 1) // 2
        return pltpu.make_async_remote_copy(
            src_ref=packed.at[target, :, part(dy)],
            dst_ref=x3.at[1 - dy, 1 - side, :, part(dy)],
            send_sem=x3_send.at[dy + 1, side, k],
            recv_sem=x3_recv.at[1 - dy, 1 - side],
            device_id=device(target, dy, dx),
            device_id_type=MESH,
        )

    late = []
    for dy in steps_y:
        for k in range(gz - 1, -1, -1):
            if (dy, k) != (0, 0):
                late.append((exists(dy, 0), functools.partial(clean_middle, dy, k)))
    for dy in steps_y:
        for dx in steps_x:
            if dx != 0:
                ok = exists(dy, dx) & (high_slab if dx > 0 else low_slab)
                for k in range(gz):
                    late.append((ok, functools.partial(clean_edge, dy, dx, k)))
    for ok, make in late:
        when(ok, lambda make=make: make().start())
    m3[1, me] = packed[me]
    for index, ok in ((0, at_y == 0), (2, at_y == gy - 1)):
        def no_row_again(index=index):
            m3[index] = jnp.zeros(m3.shape[1:], F32)
            x3[index] = jnp.zeros(x3.shape[1:], F32)
        pl.when(ok)(no_row_again)
    for side, ok in ((0, at_x == 0), (1, at_x == gx - 1)):
        def no_side(side=side):
            for index in range(3):
                x3[index, side] = jnp.zeros(x3.shape[2:], F32)
        pl.when(ok)(no_side)
    for dy in steps_y:
        for k in range(gz):
            if (dy, k) != (0, 0):
                source = peer(k)
                def await_clean(dy=dy, source=source):
                    pltpu.make_async_remote_copy(
                        src_ref=packed.at[0, :, part(-dy)],
                        dst_ref=m3.at[1 + dy, source, :, part(-dy)],
                        send_sem=m3_send.at[1 + dy, 0],
                        recv_sem=m3_recv.at[1 + dy, source],
                        device_id=device(source, dy, 0),
                        device_id_type=MESH,
                    ).wait_recv()
                when(exists(dy, 0), await_clean)
    for dy in steps_y:
        for dx in steps_x:
            if dx != 0:
                side = (dx + 1) // 2
                source = gz - 1 if dx < 0 else 0
                def await_side(dy=dy, dx=dx, side=side, source=source):
                    pltpu.make_async_remote_copy(
                        src_ref=packed.at[0, :, part(-dy)],
                        dst_ref=x3.at[1 + dy, side, :, part(-dy)],
                        send_sem=x3_send.at[1 + dy, side, 0],
                        recv_sem=x3_recv.at[1 + dy, side],
                        device_id=device(source, dy, dx),
                        device_id_type=MESH,
                    ).wait_recv()
                when(exists(dy, dx), await_side)

    for ok, make in late:
        when(ok, lambda make=make: make().wait_send())


def segment_kernel(
    sizes,
    where_ref,
    m3,
    x3,
    narrow_ref,
    wide_ref,
    in_ref,
    last_ref,
    clean_ref,
    out_ref,
    middle_ref,
    edge_ref,
    taps,
    result,
):
    gz, gy, gx = sizes
    lines, planes, bx = middle_ref.shape
    by, bz = lines - 4, planes - 4
    me, at_y, at_x = where_ref[0], where_ref[1], where_ref[2]
    slab = bx // gz
    lane = lane_of((bz + 4, LANES))
    for line in range(by + 4):
        index, y = (0, by - 2 + line) if line < 2 else (1, line - 2) if line < by + 2 else (2, line - by - 2)
        tile, off = divmod(y * slab, LANES)
        lanes = slice(tile * LANES, (tile + 1) * LANES)
        whole = jnp.zeros((bz + 4, LANES), F32)
        for source in range(gz):
            begin = source * slab
            piece = pltpu.roll(m3[index, source, :, lanes], (begin - off) % LANES, 1)
            whole = jnp.where((lane >= begin) & (lane < begin + slab), piece, whole)
        middle_ref[line] = whole
        before = pltpu.roll(x3[index, 0, :, lanes], (bx - off - slab) % LANES, 1)
        after = pltpu.roll(x3[index, 1, :, lanes], (-off) % LANES, 1)
        edge_ref[line] = jnp.where(lane < LANES // 2, after, before)

    in_left = left_rows(narrow_ref[96:144, :])
    out_left = left_rows(
        jnp.concatenate([wide_ref[48 * a + 32 : 48 * a + 48, :] for a in range(3)], axis=0)
    )
    in_bias = jnp.concatenate([column(in_ref)] * 3, axis=0)
    out_bias = column(last_ref)
    for y in range(by + 2):
        taps[y, pl.ds(15, planes, stride=16), :] = jnp.zeros((planes, bx), F32)
    lane = lane_of((planes, bx))
    for line in range(lines):
        middle, edge = middle_ref[line], edge_ref[line]
        for s in range(5):
            value = middle
            if s < 2:
                value = pltpu.roll(jnp.where(lane >= bx - (2 - s), edge, middle), 2 - s, 1)
            if s > 2:
                value = pltpu.roll(jnp.where(lane < s - 2, edge, middle), bx - (s - 2), 1)
            for b in range(3):
                if 0 <= line - b < by + 2:
                    taps[line - b, pl.ds(b * 5 + s, planes, stride=16), :] = value

    for z in range(bz):
        clean_ref[z] = middle_ref[2 : 2 + by, 2 + z, :]
    shape = (48, (by + 2) * bx)
    lane, row = lane_of(shape), row_of(shape)
    place_y = at_y * by + lane // bx - 1
    place_x = at_x * bx + lane % bx + row // 16 - 1
    inside = (place_y >= 0) & (place_y < gy * by) & (place_x >= 0) & (place_x < gx * bx)
    mask = jnp.where(inside, 1.0, 0.0).astype(F32)
    partial = []
    for z in range(bz + 2):
        rows = jnp.concatenate([taps[y, z * 16 : z * 16 + 48, :] for y in range(by + 2)], axis=1)
        high, low = split(rows)
        grown = jnp.maximum(mxu(in_left, right_rows(high, low)) + in_bias, 0.0) * mask
        if z == 0:
            grown = grown * jnp.where(me > 0, 1.0, 0.0).astype(F32)
        if z == bz + 1:
            grown = grown * jnp.where(me < gz - 1, 1.0, 0.0).astype(F32)
        high, low = split(grown)
        field_high = jnp.concatenate([high[:, b * bx : (b + by) * bx] for b in range(3)], axis=0)
        field_low = jnp.concatenate([low[:, b * bx : (b + by) * bx] for b in range(3)], axis=0)
        partial.append(mxu(out_left, right_rows(field_high, field_low)))
        if z >= 2:
            total = partial[z - 2][0:16] + partial[z - 1][16:32] + partial[z][32:48] + out_bias
            for y in range(by):
                result[pl.ds((z - 2) * by + y, 16, stride=bz * by), :] = total[:, y * bx : (y + 1) * bx]
    out_ref[...] = result[0 : 16 * bz * by, :]


def narrow_rows(weight):
    parts = weight.shape[0] // 16
    kernel = weight.reshape(parts, 16, 3, 3, 3)
    moved = jnp.stack(
        [jnp.pad(kernel, ((0, 0),) * 4 + ((c, 2 - c),)) for c in range(3)], axis=1
    ).reshape(parts * 48, 3, 15)
    return jnp.pad(moved, ((0, 0), (0, 0), (0, 1))).reshape(parts * 48, 48)


def wide_rows(weight):
    outs, ins = weight.shape[0], weight.shape[1]
    return weight.reshape(outs, ins, 3, 9).transpose(2, 0, 3, 1).reshape(3 * outs, 9 * ins)


def body(sizes, noisy, first_weight, first_bias, second_weight, second_bias, head_weight,
         seg_weight_in, seg_bias_in, seg_weight_out, seg_bias_out):
    gz, gy, gx = sizes
    bz, by, bx = noisy.shape
    depth = gz * bz
    slab = bx // gz
    tiles = -(-(by + 2) * slab // LANES)
    out_lanes = by * slab
    out_tiles = -(-out_lanes // LANES)
    narrow = narrow_rows(jnp.concatenate([first_weight, seg_weight_in], axis=0))
    wide = wide_rows(jnp.concatenate([second_weight, seg_weight_out], axis=0))
    rows = [v.reshape(1, -1) for v in (first_bias, second_bias, head_weight, seg_bias_in, seg_bias_out)]
    vmem = pl.BlockSpec(memory_space=pltpu.VMEM)
    dma = pltpu.SemaphoreType.DMA
    smem = pl.BlockSpec(memory_space=pltpu.SMEM)
    blocks = jax.ShapeDtypeStruct((gz, bz * by, bx), F32)
    halos = jax.ShapeDtypeStruct((2, gz, bz * 2, bx), F32)
    m1, x1, my, xy, where = pl.pallas_call(
        functools.partial(gather_kernel, sizes, by),
        out_shape=[blocks, blocks, halos, halos, jax.ShapeDtypeStruct((3,), jnp.int32)],
        in_specs=[vmem],
        out_specs=[vmem] * 4 + [smem],
        scratch_shapes=[
            pltpu.VMEM((2, bz * 2, bx), F32), dma((3, gz)), dma((3, gz)), dma((3, 2)), dma((3, gz))
        ],
        compiler_params=pltpu.CompilerParams(collective_id=0, has_side_effects=True),
        name="gather",
    )(noisy.reshape(bz * by, bx))
    packed = pl.pallas_call(
        functools.partial(layers_kernel, sizes, (bz, by, bx)),
        out_shape=jax.ShapeDtypeStruct((gz, bz + 4, out_tiles * LANES), F32),
        in_specs=[smem] + [vmem] * 9,
        out_specs=vmem,
        scratch_shapes=[
            pltpu.VMEM((tiles, (depth + 2) * 16, LANES), F32),
            pltpu.VMEM((tiles, (depth + 2) * 16, LANES), BF16),
            pltpu.VMEM((tiles, (depth + 2) * 16, LANES), BF16),
            pltpu.VMEM((depth + 2, 96, out_lanes), F32),
            pltpu.VMEM((depth + 16, out_tiles * LANES), F32),
        ],
        name="layers",
    )(
        where,
        m1.reshape(depth * by, bx),
        x1.reshape(depth * by, bx),
        my.reshape(2, depth * 2, bx),
        xy.reshape(2, depth * 2, bx),
        narrow,
        wide,
        *rows[:3],
    )
    m3, x3 = pl.pallas_call(
        functools.partial(scatter_kernel, sizes, by, slab),
        out_shape=[
            jax.ShapeDtypeStruct((3, gz, bz + 4, out_tiles * LANES), F32),
            jax.ShapeDtypeStruct((3, 2, bz + 4, out_tiles * LANES), F32),
        ],
        in_specs=[vmem],
        out_specs=[vmem] * 2,
        scratch_shapes=[dma((3, gz)), dma((3, gz)), dma((3, 2, gz)), dma((3, 2))],
        compiler_params=pltpu.CompilerParams(collective_id=1, has_side_effects=True),
        name="scatter",
    )(packed)
    clean, features = pl.pallas_call(
        functools.partial(segment_kernel, sizes),
        out_shape=[
            jax.ShapeDtypeStruct((bz, by, bx), F32),
            jax.ShapeDtypeStruct((16 * bz * by, bx), F32),
        ],
        in_specs=[smem] + [vmem] * 6,
        out_specs=[vmem] * 2,
        scratch_shapes=[
            pltpu.VMEM((by + 4, bz + 4, bx), F32),
            pltpu.VMEM((by + 4, bz + 4, bx), F32),
            pltpu.VMEM((by + 2, (bz + 5) * 16, bx), F32),
            pltpu.VMEM((17 * bz * by, bx), F32),
        ],
        name="segment",
    )(where, m3, x3, narrow, wide, *rows[3:])
    return clean, features.reshape(16, bz, by, bx)


def solution(mesh):
    sizes = (mesh.shape["gz"], mesh.shape["gy"], mesh.shape["gx"])
    in_specs = (P(("win", "gz"), "gy", "gx"), P(), P(), P(), P(), P(), P(), P(), P(), P())
    out_specs = (P(("win", "gz"), "gy", "gx"), P(None, ("win", "gz"), "gy", "gx"))
    return jax.shard_map(
        functools.partial(body, sizes), mesh=mesh, in_specs=in_specs, out_specs=out_specs, check_vma=False
    )
```
